32 devices in a mesh: dp: 4 (over z), row: 2 (over y), col: 4 (over x, core).
Axes of the slice: x: 2, y: 2, z: 4, core: 2. Of those that a mesh axis runs over, the one named last changes fastest.
Arguments:
- tokens: bfloat16 [1024, 8192], P('dp', 'row'), may hold values from -6 to 6
- w_up: bfloat16 [64, 16, 128, 128], P('row', 'col'), may hold values from -0.1875 to 0.1875
- w_down: bfloat16 [64, 16, 128, 128], P('row', 'col'), may hold values from -0.125 to 0.125
- kept_cols: int32 [64, 16], P('row', 'col'), may hold values from 0 to 31, as said below
- grad_out: bfloat16 [1024, 8192], P('dp', 'row'), may hold values from -6 to 6
Outputs:
- output: bfloat16 [1024, 8192], P('dp', 'row')
- grad_in: bfloat16 [1024, 8192], P('dp', 'row')
- grad_up: float32 [64, 16, 128, 128], P('row', 'col', 'dp')
- grad_down: float32 [64, 16, 128, 128], P('row', 'col', 'dp')
The draws below stay inside these ranges and needn't reach their ends.
Inputs may be any that keep to these rules, and one draw needn't show every extreme that they name: `kept_cols`: for each block row r and each group j of the 4 groups of block columns, the entries j * 4 to j * 4 + 3 of row r are distinct.
All inputs are finite; a program needn't handle non-finite values.
Results may differ from the reference program's by a relative error of at most 0.015.
Values may be sent and summed in bfloat16 or wider, within the bound.
No kernel may reach another device: no remote copies, remote signals or barrier semaphores. Data moves between devices by JAX's collectives and lax.ppermute only.
A program may use at most 128 MiB of HBM per device.

```python
import jax
import jax.numpy as jnp
from jax import lax

D = 8192
BLK = 128
TOK = 256
RB = 64
CB = 128
KEEP = 16
KS = 4
TOKENS = 1024
N_DP = 4
N_ROW = 2
N_COL = 4


def draw_kept_cols(key, part):
    shard_columns = CB // N_COL
    scores = jax.random.randint(key, (RB, N_COL, shard_columns), 0, 1048576, dtype=jnp.int32)
    distinct = scores * shard_columns + jnp.arange(shard_columns, dtype=jnp.int32)[None, None, :]
    order = jnp.argsort(distinct, axis=-1, stable=True).astype(jnp.int32)
    return order[:, :, :KS].reshape(RB, KEEP)


def levels(stream_key, shape, shards, low, top_value):
    gain = 1.0
    for dim, shards_of in shards:
        heights = jax.random.uniform(jax.random.fold_in(jax.random.fold_in(stream_key, 6), dim), (shards_of,), jnp.float32, low / len(shards), top_value / len(shards))
        gain = gain * jnp.repeat(jnp.exp(heights), shape[dim] // shards_of).reshape((-1,) + (1,) * (len(shape) - 1 - dim))
    return gain


def scatter_about(stream_key, shape, scale, limit, shards=(), held_as=jnp.bfloat16):
    values = scale * jax.random.normal(stream_key, shape, jnp.float32)
    if shards:
        values = values * levels(stream_key, shape, shards, -0.22, 0.18)
    return jnp.clip(values, -limit, limit).astype(held_as)


def setup_inputs(seed: int = 0) -> dict:
    arg_keys = jax.random.split(jax.random.key(seed), 6)
    return {
        "tokens": scatter_about(arg_keys[0], (TOKENS, D), 1.0, 6.0, ((0, 4), (1, 2))),
        "w_up": scatter_about(arg_keys[1], (RB, KEEP, BLK, BLK), (D // 8) ** -0.5, 0.1875, ((0, 2), (1, 4))),
        "w_down": scatter_about(arg_keys[2], (RB, KEEP, BLK, BLK), (KEEP * BLK) ** -0.5, 0.125, ((0, 2), (1, 4))),
        "kept_cols": draw_kept_cols(jax.random.fold_in(arg_keys[5], 71), 0),
        "grad_out": scatter_about(arg_keys[4], (TOKENS, D), 1.0, 6.0, ((0, 4), (1, 2))),
    }


CURVE = 0.7978845608028654
CUBIC = 0.044715


def activate(field):
    inside = CURVE * (field + CUBIC * field * field * field)
    tangent = jnp.tanh(inside)
    result = 0.5 * field * (1.0 + tangent)
    steepness = 0.5 * (1.0 + tangent) + 0.5 * field * (1.0 - tangent * tangent) * CURVE * (1.0 + 3.0 * CUBIC * field * field)
    return result, steepness


def through_bf16(field):
    rounded = lax.optimization_barrier(field.astype(jnp.bfloat16))
    return rounded.astype(jnp.float32)


def reference(tokens, w_up, w_down, kept_cols, grad_out):
    block_width = w_up.shape[2]
    block_rows = w_up.shape[0]
    slot_count = w_up.shape[1]
    per_device = block_rows // N_ROW
    group_start = (jnp.arange(slot_count, dtype=jnp.int32) // KS) * (CB // N_COL)
    column_ids = (kept_cols + group_start[None, :]).astype(jnp.int32)
    group_ids = column_ids.reshape(N_ROW, per_device * slot_count)
    flat_ids = column_ids.reshape(-1)
    up_wide = w_up.astype(jnp.float32)
    down_wide = w_down.astype(jnp.float32)
    factor = float(TOKENS) ** -0.5

    def row_sums(blocks):
        grouped = blocks.reshape(TOK, N_ROW, per_device * slot_count, block_width)
        moved = jnp.transpose(grouped, (1, 2, 0, 3))

        def one_group(pieces, indices):
            return jax.ops.segment_sum(pieces, indices, num_segments=CB)

        sums = jax.vmap(one_group)(moved, group_ids)
        total = jnp.sum(through_bf16(sums), axis=0)
        return jnp.transpose(total, (1, 0, 2)).reshape(TOK, CB * block_width)

    def pick(field):
        reshaped = field.reshape(TOK, CB, block_width)
        picked = jnp.take(reshaped, flat_ids, axis=1)
        return picked.reshape(TOK, block_rows, slot_count, block_width).astype(jnp.float32)

    def one_step(carry, group):
        tok_group, grad_group = group
        tok_cube = tok_group.reshape(TOK, block_rows, block_width).astype(jnp.float32)
        grad_cube = grad_group.reshape(TOK, block_rows, block_width).astype(jnp.float32)
        hidden = row_sums(jnp.einsum("trb,rkbf->trkf", tok_cube, up_wide))
        act_value, act_slope = activate(hidden)
        act = act_value.astype(jnp.bfloat16)
        slope = act_slope.astype(jnp.bfloat16)
        act_picked = pick(act)
        output = jnp.einsum("trkf,rkfd->trd", act_picked, down_wide).reshape(TOK, D).astype(jnp.bfloat16)
        grad_act = row_sums(jnp.einsum("trd,rkfd->trkf", grad_cube, down_wide))
        grad_hidden = (grad_act * slope.astype(jnp.float32)).astype(jnp.bfloat16)
        grad_picked = pick(grad_hidden)
        grad_in = jnp.einsum("trkf,rkbf->trb", grad_picked, up_wide).reshape(TOK, D).astype(jnp.bfloat16)
        part_up = through_bf16(factor * jnp.einsum("trb,trkf->rkbf", tok_cube, grad_picked))
        part_down = through_bf16(factor * jnp.einsum("trkf,trd->rkfd", act_picked, grad_cube))
        return (carry[0] + part_up, carry[1] + part_down), (output, grad_in)

    zeros = jnp.zeros((block_rows, slot_count, block_width, block_width), jnp.float32)
    tok_groups = tokens.reshape(N_DP, TOK, D)
    grad_groups = grad_out.reshape(N_DP, TOK, D)
    totals, results = lax.scan(one_step, (zeros, zeros), (tok_groups, grad_groups))
    output = results[0].reshape(TOKENS, D)
    grad_in = results[1].reshape(TOKENS, D)
    return (output, grad_in, totals[0], totals[1])
```

```python
import functools

import jax
import jax.numpy as jnp
from jax import lax
from jax.experimental import pallas as pl
from jax.experimental.pallas import tpu as pltpu
from jax.sharding import PartitionSpec as P


FF = 16384


CURVE = 0.7978845608028654
CUBIC = 0.044715


F32 = jnp.float32
BF16 = jnp.bfloat16


def activate(field):
    inside = CURVE * (field + CUBIC * field * field * field)
    tangent = jnp.tanh(inside)
    result = 0.5 * field * (1.0 + tangent)
    steepness = 0.5 * (1.0 + tangent) + 0.5 * field * (1.0 - tangent * tangent) * CURVE * (
        1.0 + 3.0 * CUBIC * field * field
    )
    return (result, steepness)


def column_lookup(kept_cols, columns):
    flattened = kept_cols.reshape(-1)
    return (flattened[:, None] == jnp.arange(columns, dtype=jnp.int32)[None, :]).astype(jnp.float32)


def spread_columns(blocks, lookup):
    row_count = blocks.shape[0]
    flattened = blocks.reshape(row_count, lookup.shape[0], blocks.shape[3])
    spread = jnp.einsum("tsf,sc->tcf", flattened, lookup, precision=lax.Precision.HIGHEST)
    return spread.reshape(row_count, -1)


def pick_columns(field, kept_cols, block_width):
    row_count = field.shape[0]
    reshaped = field.reshape(row_count, -1, block_width)
    picked = jnp.take(reshaped, kept_cols.reshape(-1), axis=1)
    return picked.reshape(row_count, kept_cols.shape[0], kept_cols.shape[1], block_width)


def on_any_mesh(tokens, w_up, w_down, kept_cols, grad_out):
    block_width = w_up.shape[2]
    token_count = tokens.shape[0]
    block_rows = w_up.shape[0]
    shard_columns = FF // (block_width * lax.axis_size("col"))
    tokens_cube = tokens.reshape(token_count, block_rows, block_width)
    grad_cube = grad_out.reshape(token_count, block_rows, block_width)
    lookup = column_lookup(kept_cols, shard_columns)
    factor = float(token_count * lax.axis_size("dp")) ** (-0.5)
    blocks = jnp.einsum("trb,rkbf->trkf", tokens_cube, w_up, preferred_element_type=jnp.float32)
    hidden_share = lax.psum_scatter(
        spread_columns(blocks, lookup).astype(jnp.bfloat16), "row", scatter_dimension=0, tiled=True
    ).astype(jnp.float32)
    act_value, act_slope = activate(hidden_share)
    act_share = act_value.astype(jnp.bfloat16)
    slope_share = act_slope.astype(jnp.bfloat16)
    act_all, slope_all = (
        lax.all_gather(act_share, "row", axis=0, tiled=True),
        lax.all_gather(slope_share, "row", axis=0, tiled=True),
    )
    act_picked = pick_columns(act_all, kept_cols, block_width)
    out_term = jnp.einsum("trkf,rkfd->trd", act_picked, w_down, preferred_element_type=jnp.float32)
    output = lax.psum(out_term.reshape(token_count, -1).astype(jnp.bfloat16), "col")
    back_blocks = jnp.einsum(
        "trd,rkfd->trkf", grad_cube, w_down, preferred_element_type=jnp.float32
    )
    back_all = lax.psum(spread_columns(back_blocks, lookup).astype(jnp.bfloat16), "row").astype(
        jnp.float32
    )
    hidden_grad = (back_all * slope_all).astype(jnp.bfloat16)
    grad_picked = pick_columns(hidden_grad, kept_cols, block_width)
    in_term = jnp.einsum("trkf,rkbf->trb", grad_picked, w_up, preferred_element_type=jnp.float32)
    grad_in = lax.psum(in_term.reshape(token_count, -1).astype(jnp.bfloat16), "col")
    up_weights = factor * jnp.einsum(
        "trb,trkf->rkbf", tokens_cube, grad_picked, preferred_element_type=jnp.float32
    )
    down_weights = factor * jnp.einsum(
        "trkf,trd->rkfd", act_picked, grad_cube, preferred_element_type=jnp.float32
    )
    grad_up, grad_down = (
        lax.psum_scatter(
            up_weights.astype(jnp.bfloat16), "dp", scatter_dimension=2, tiled=True
        ).astype(jnp.float32),
        lax.psum_scatter(
            down_weights.astype(jnp.bfloat16), "dp", scatter_dimension=2, tiled=True
        ).astype(jnp.float32),
    )
    return (output, grad_in, grad_up, grad_down)


QUARTERS = 4
DP, CORE, COL, FAR, OUTER = range(5)
NN = (((1,), (0,)), ((), ()))
NT = (((1,), (1,)), ((), ()))


def dot(left, right, dims):
    return lax.dot_general(left, right, dims, preferred_element_type=F32)


def across(blocks):
    return jnp.concatenate([blocks[k] for k in range(blocks.shape[0])], axis=1)


def stacked(blocks):
    return blocks.reshape(blocks.shape[0] * blocks.shape[1], blocks.shape[2])


def whole_block(shape):
    return pl.BlockSpec(shape, lambda *_: (0,) * len(shape))


def call(kernel, grid, scalars, inputs, in_specs, out_shape, out_specs, scratch=()):
    return pl.pallas_call(
        kernel,
        out_shape=out_shape,
        grid_spec=pltpu.PrefetchScalarGridSpec(
            num_scalar_prefetch=len(scalars),
            grid=grid,
            in_specs=in_specs,
            out_specs=out_specs,
            scratch_shapes=list(scratch),
        ),
    )(*scalars, *inputs)


def spread_kernel(transposed, step, kept, place, x_ref, w_ref, *rest):
    outs, total = rest[:-1], rest[-1]
    slots, width = w_ref.shape[1], w_ref.shape[2]
    quarter = width // QUARTERS
    at = pl.program_id(0)

    @pl.when(at == 0)
    def _():
        total[...] = jnp.zeros_like(total)

    def row(i, carry):
        x = x_ref[:, pl.ds(pl.multiple_of(i * width, width), width)]
        if transposed:
            terms = dot(x, stacked(w_ref[i]), NT)
        else:
            terms = dot(x, across(w_ref[i]), NN)
        for k in range(slots):
            column = kept[(at * step + i) * slots + k]
            total[column] += terms[:, k * width:(k + 1) * width]
        return carry

    lax.fori_loop(0, step, row, 0, unroll=4)

    @pl.when(at == pl.num_programs(0) - 1)
    def _():
        def flip(column, carry):
            turned = total[column].astype(BF16).T
            quarters = [turned[q * quarter:(q + 1) * quarter] for q in range(QUARTERS)]
            if transposed:
                for q in range(QUARTERS):
                    outs[q][column] = quarters[q]
            else:
                far = place[FAR]
                outs[0][far, column] = quarters[0]
                outs[0][1 - far, column] = quarters[3]
                outs[1][far, column] = quarters[1]
                outs[1][1 - far, column] = quarters[2]
            return carry

        lax.fori_loop(0, total.shape[0], flip, 0, unroll=8)


def spread(kept, place, x, w, columns, transposed, step=8):
    rows, slots, width = w.shape[0], w.shape[1], w.shape[2]
    tokens = x.shape[0]
    shape = (columns, width // QUARTERS, tokens)
    shapes = [shape] * QUARTERS if transposed else [(2,) + shape] * 2
    return call(
        functools.partial(spread_kernel, transposed, step),
        (rows // step,),
        (kept, place),
        (x, w),
        [
            pl.BlockSpec((tokens, step * width), lambda g, *_: (0, g)),
            pl.BlockSpec((step, slots, width, width), lambda g, *_: (g, 0, 0, 0)),
        ],
        [jax.ShapeDtypeStruct(shape, BF16) for shape in shapes],
        [whole_block(shape) for shape in shapes],
        [pltpu.VMEM((columns, tokens, width), F32)],
    )


def activate_kernel(own_ref, sent_ref, near_ref, far_ref, near_slope, far_slope):
    for i, (act_ref, slope_ref) in enumerate(((near_ref, near_slope), (far_ref, far_slope))):
        act, slope = activate(own_ref[i].astype(F32) + sent_ref[i].astype(F32))
        act_ref[...] = act.astype(BF16)
        slope_ref[...] = slope.astype(BF16)


def activate_pair(own, sent, step=8):
    _, columns, quarter, tokens = own.shape
    pair = pl.BlockSpec((2, step, quarter, tokens), lambda g: (0, g, 0, 0))
    one = pl.BlockSpec((step, quarter, tokens), lambda g: (g, 0, 0))
    return call(
        activate_kernel,
        (columns // step,),
        (),
        (own, sent),
        [pair, pair],
        [jax.ShapeDtypeStruct((columns, quarter, tokens), BF16)] * 4,
        [one] * 4,
    )


def gather_kernel(transposed, mirrored, step, kept, place, *rest):
    parts, w_ref, keep_ref, send_ref, natural = (
        rest[:QUARTERS], rest[QUARTERS], rest[-3], rest[-2], rest[-1]
    )
    slots, width = w_ref.shape[1], w_ref.shape[2]
    half = keep_ref.shape[0]
    at = pl.program_id(0)

    def lay(order):
        def flip(column, carry):
            natural[column] = jnp.concatenate([part[column] for part in order], axis=0).T
            return carry

        lax.fori_loop(0, natural.shape[0], flip, 0, unroll=8)

    if mirrored:
        pl.when((at == 0) & (place[FAR] == 0))(lambda: lay(parts))
        pl.when((at == 0) & (place[FAR] == 1))(lambda: lay(parts[::-1]))
    else:
        pl.when(at == 0)(lambda: lay(parts))

    mine = pl.multiple_of(place[CORE] * half, half)
    other = pl.multiple_of((1 - place[CORE]) * half, half)

    def row(i, carry):
        columns = [kept[(at * step + i) * slots + k] for k in range(slots)]
        lanes = pl.ds(pl.multiple_of(i * width, width), width)
        for ref, start in ((keep_ref, mine), (send_ref, other)):
            left = jnp.concatenate([natural[c, pl.ds(start, half), :] for c in columns], axis=1)
            if transposed:
                term = dot(left, across(w_ref[i]), NT)
            else:
                term = dot(left, stacked(w_ref[i]), NN)
            ref[:, lanes] = term.astype(BF16)
        return carry

    lax.fori_loop(0, step, row, 0, unroll=4)


def gather(kept, place, parts, w, transposed, mirrored, step=8):
    rows, slots, width = w.shape[0], w.shape[1], w.shape[2]
    columns, quarter, tokens = parts[0].shape
    half = tokens // 2
    return call(
        functools.partial(gather_kernel, transposed, mirrored, step),
        (rows // step,),
        (kept, place),
        (*parts, w),
        [whole_block((columns, quarter, tokens))] * QUARTERS
        + [pl.BlockSpec((step, slots, width, width), lambda g, *_: (g, 0, 0, 0))],
        [jax.ShapeDtypeStruct((half, rows * width), BF16)] * 2,
        [pl.BlockSpec((half, step * width), lambda g, *_: (0, g))] * 2,
        [pltpu.VMEM((columns, tokens, width), BF16)],
    )


def up_weights_kernel(factor, q, direct, step, kept, place, own, sent, near, far, tok_ref, *outs):
    grad_ref, outs = outs[0], outs[1:]
    quarter = grad_ref.shape[1]
    slots = outs[0].shape[-1] // quarter
    at = pl.program_id(0)

    def hidden_grad(slope):
        def block(c, carry):
            grad = (own[c].astype(F32) + sent[c].astype(F32)) * slope[c].astype(F32)
            grad_ref[c] = grad.astype(BF16)
            return carry

        lax.fori_loop(0, own.shape[0], block, 0, unroll=4)

    swapped = 0 if q < 2 else 1
    pl.when((at == 0) & (place[FAR] == swapped))(lambda: hidden_grad(near))
    pl.when((at == 0) & (place[FAR] != swapped))(lambda: hidden_grad(far))

    if direct:
        owners = [jnp.bitwise_xor(place[DP], m) for m in range(QUARTERS)]
    else:
        owners = [jnp.where(place[FAR] == 0, m, 3 - m) for m in range(QUARTERS)]

    def row(i, carry):
        left = jnp.concatenate(
            [tok_ref[i, pl.ds(pl.multiple_of(m * quarter, quarter), quarter), :] for m in owners],
            axis=0,
        )
        right = jnp.concatenate(
            [grad_ref[kept[(at * step + i) * slots + k]] for k in range(slots)], axis=0
        )
        term = (factor * dot(left, right, NT)).astype(BF16)
        pieces = [term[m * quarter:(m + 1) * quarter] for m in range(QUARTERS)]
        outs[0][i] = pieces[0]
        for m in (1, 2, 3):
            if direct:
                outs[m][i] = pieces[m]
            else:
                outs[1][m - 1, i] = pieces[m]
        return carry

    lax.fori_loop(0, step, row, 0, unroll=4)


def up_weights(kept, place, q, direct, own, sent, near, far, tok_t, slots, factor, step=16):
    columns, quarter, tokens = own.shape
    rows, width = tok_t.shape[0], tok_t.shape[1]
    one = (rows, quarter, slots * quarter)
    one_spec = pl.BlockSpec((step,) + one[1:], lambda g, *_: (g, 0, 0))
    three_spec = pl.BlockSpec((3, step) + one[1:], lambda g, *_: (0, g, 0, 0))
    shapes = [one] * 4 if direct else [one, (3,) + one]
    return call(
        functools.partial(up_weights_kernel, factor, q, direct, step),
        (rows // step,),
        (kept, place),
        (own, sent, near, far, tok_t),
        [whole_block((columns, quarter, tokens))] * 4
        + [pl.BlockSpec((step, width, tokens), lambda g, *_: (g, 0, 0))],
        [jax.ShapeDtypeStruct((columns, quarter, tokens), BF16)]
        + [jax.ShapeDtypeStruct(shape, BF16) for shape in shapes],
        [whole_block((columns, quarter, tokens))]
        + ([one_spec] * 4 if direct else [one_spec, three_spec]),
    )


def join_kernel(kinds, place, *rest):
    terms, out_ref = rest[:-1], rest[-1]
    step, slots, quarter, width = out_ref.shape
    lane = lax.broadcasted_iota(jnp.int32, (quarter, width), 1) // quarter
    outer = place[OUTER] == 1

    def row(i, carry):
        sums, first = [], 0
        for direct in kinds:
            group = [term[i].astype(F32) for term in terms[first:first + 4]]
            first += 4
            if direct:
                sums.append(group[0] + group[1] + group[2] + group[3])
            else:
                sums.append(jnp.where(outer, group[0] + group[1], group[2] + group[3]))
        for k in range(slots):
            block = None
            for q in range(QUARTERS):
                shift = ((q - k) * quarter) % width
                piece = pltpu.roll(sums[q], shift, 1) if shift else sums[q]
                block = piece if block is None else jnp.where(lane == q, piece, block)
            out_ref[i, k] = block
        return carry

    lax.fori_loop(0, step, row, 0, unroll=4)


def join(place, kinds, parts, slots, step=8):
    rows, quarter, width = parts[0][0].shape
    terms = [term for part in parts for term in part]

    def spec(term):
        if len(term.shape) == 4:
            return pl.BlockSpec((None, step, quarter, width), lambda g, *_: (0, g, 0, 0))
        return pl.BlockSpec((step, quarter, width), lambda g, *_: (g, 0, 0))

    return call(
        functools.partial(join_kernel, kinds),
        (rows // step,),
        (place,),
        terms,
        [spec(term) for term in terms],
        jax.ShapeDtypeStruct((rows, slots, quarter, width), F32),
        pl.BlockSpec((step, slots, quarter, width), lambda g, *_: (g, 0, 0, 0)),
    )


def down_weights_kernel(factor, step, kept, place, *rest):
    ends, inner, own_ref, pieces, out_ref, wide = (
        rest[:4], rest[4:8], rest[8], rest[9:13], rest[13], rest[14]
    )
    columns, quarter, tokens = ends[0].shape
    slots, width = out_ref.shape[1], out_ref.shape[3]
    m, at = pl.program_id(0), pl.program_id(1)
    start = (jnp.bitwise_xor(place[COL], m) * pl.num_programs(1) + at) * step

    def lay(acts):
        def block(column, carry):
            for d in range(4):
                wide[column, :, d * tokens:(d + 1) * tokens] = acts[d][column]
            return carry

        lax.fori_loop(0, columns, block, 0, unroll=2)

    opening = (m == 0) & (at == 0)
    pl.when(opening & (place[OUTER] == 1))(lambda: lay(ends))
    pl.when(opening & (place[OUTER] == 0))(lambda: lay(inner))

    def work(piece):
        def row(i, carry):
            lanes = pl.ds(pl.multiple_of(i * width, width), width)
            left = jnp.concatenate(
                [wide[kept[(start + i) * slots + k]] for k in range(slots)], axis=0
            )
            right = jnp.concatenate(
                [own_ref[:, lanes]] + [piece[d, :, lanes] for d in range(3)], axis=0
            )
            out_ref[i] = (factor * dot(left, right, NN)).reshape(slots, quarter, width)
            return carry

        lax.fori_loop(0, step, row, 0, unroll=2)

    for index, piece in enumerate(pieces):
        pl.when(m == index)(functools.partial(work, piece))


def down_weights(kept, place, ends, inner, own, pieces, slots, factor, step=8):
    columns, quarter, tokens = ends[0].shape
    width = slots * quarter
    rows = own.shape[1] // width
    steps = rows // (len(pieces) * step)

    def own_index(m, g, kept, place):
        return (0, jnp.bitwise_xor(place[COL], m) * steps + g)

    def out_index(m, g, kept, place):
        return (jnp.bitwise_xor(place[COL], m) * steps + g, 0, 0, 0)

    def piece_index(index):
        def of(m, g, kept, place):
            return (0, 0, jnp.where(m < index, 0, jnp.where(m > index, steps - 1, g)))

        return of

    return call(
        functools.partial(down_weights_kernel, factor, step),
        (len(pieces), steps),
        (kept, place),
        (*ends, *inner, own, *pieces),
        [whole_block((columns, quarter, tokens))] * 8
        + [pl.BlockSpec((tokens, step * width), own_index)]
        + [pl.BlockSpec((3, tokens, step * width), piece_index(i)) for i in range(len(pieces))],
        jax.ShapeDtypeStruct((rows, slots, quarter, width), F32),
        pl.BlockSpec((step, slots, quarter, width), out_index),
        [pltpu.VMEM((columns, quarter, 4 * tokens), BF16)],
    )


def seat_kernel(place, mine_ref, other_ref, out_ref):
    pl.when(pl.program_id(0) == 0)(lambda: out_ref.__setitem__(..., mine_ref[...]))
    pl.when(pl.program_id(0) == 1)(lambda: out_ref.__setitem__(..., other_ref[...]))


def seat(place, mine, other):
    half, width = mine.shape
    return call(
        seat_kernel,
        (2,),
        (place,),
        (mine, other),
        [whole_block((half, width))] * 2,
        jax.ShapeDtypeStruct((2 * half, width), BF16),
        pl.BlockSpec(
            (half, width), lambda g, place: (jnp.bitwise_xor(place[CORE], g), 0)
        ),
    )


def swap(mask, size):
    return [(i, i ^ mask) for i in range(size)]


INWARD = [(0, 1), (3, 2)]
OUTWARD = [(1, 0), (2, 3)]
MIDDLE = [(1, 2), (2, 1)]


def plus(a, b):
    return (a.astype(F32) + b.astype(F32)).astype(BF16)


def on_device(tokens, w_up, w_down, kept_cols, grad_out):
    return layer(tokens, w_up, w_down, kept_cols, grad_out)


def layer(tokens, w_up, w_down, kept_cols, grad_out):
    width = w_up.shape[2]
    token_count = tokens.shape[0]
    rows, slots = w_up.shape[0], w_up.shape[1]
    columns = FF // (width * lax.axis_size("col"))
    factor = float(token_count * lax.axis_size("dp")) ** (-0.5)
    dp, col = lax.axis_index("dp"), lax.axis_index("col")
    far = dp // 2
    outer = jnp.where((dp == 0) | (dp == 3), 1, 0)
    kept = kept_cols.reshape(-1)
    place = jnp.stack([dp, col % 2, col, far, outer]).astype(jnp.int32)

    share = grad_out.shape[1] // 4
    mine = lax.dynamic_slice_in_dim(grad_out, col * share, share, axis=1)
    beside = lax.ppermute(mine, "dp", swap(1, 4))

    ends_own, inner_own = spread(kept, place, tokens, w_up, columns, False)
    ends_sent = lax.ppermute(ends_own, "row", swap(1, 2))
    middle = lax.ppermute(jnp.stack([mine, beside]), "dp", MIDDLE)
    back_own = spread(kept, place, grad_out, w_down, columns, True)
    back_sent = {}
    for q in (0, 3):
        back_sent[q] = lax.ppermute(back_own[q], "row", swap(1, 2))
    inner_sent = lax.ppermute(inner_own, "row", swap(1, 2))
    for q in (1, 2):
        back_sent[q] = lax.ppermute(back_own[q], "row", swap(1, 2))
    tok_t = tokens.reshape(token_count, rows, width).transpose(1, 2, 0)

    end_near, end_far, end_near_slope, end_far_slope = activate_pair(ends_own, ends_sent)
    ends = [
        end_near,
        lax.ppermute(end_near, "dp", OUTWARD),
        lax.ppermute(end_far, "dp", [(2, 0), (1, 3)]),
        lax.ppermute(end_far, "dp", [(3, 0), (0, 3)]),
    ]

    grad, up_terms = {}, {}

    def weights_of(q, direct):
        slopes = (end_near_slope, end_far_slope) if q in (0, 3) else (near_slope, far_slope)
        grad[q], *terms = up_weights(
            kept, place, q, direct, back_own[q], back_sent[q], *slopes, tok_t, slots, factor
        )
        if direct:
            return [terms[0]] + [lax.ppermute(terms[m], "dp", swap(m, 4)) for m in (1, 2, 3)]
        home, rest = terms
        arrived = lax.ppermute(rest, "dp", INWARD)
        return home, rest, arrived

    def second_of(home, rest, arrived):
        near = plus(rest[0], arrived[0])
        return home, near, lax.ppermute(plus(rest[1:], arrived[1:]), "dp", MIDDLE)

    def third_of(home, near, crossed):
        last = lax.ppermute(plus(home, crossed[1]), "dp", OUTWARD)
        return [home, last, near, crossed]

    stage = {}
    stage[0] = weights_of(0, False)
    reach = lax.ppermute(middle, "dp", OUTWARD)
    beyond = jnp.where(outer == 1, reach, middle)
    stage[3] = weights_of(3, False)
    stage[0] = second_of(*stage[0])
    piece = jnp.concatenate([beside[None], beyond], axis=0)
    piece_chip = lax.ppermute(piece, "col", swap(2, 4))
    piece_core = lax.ppermute(piece, "col", swap(1, 4))
    up_terms[0] = third_of(*stage[0])
    stage[3] = second_of(*stage[3])

    near, far_act, near_slope, far_slope = activate_pair(inner_own, inner_sent)
    inner = [
        near,
        lax.ppermute(near, "dp", INWARD),
        lax.ppermute(far_act, "dp", MIDDLE),
        lax.ppermute(far_act, "dp", [(3, 1), (0, 2)]),
    ]
    keep, send = gather(kept, place, [end_near, near, far_act, end_far], w_down, False, True)
    half = plus(keep, lax.ppermute(send, "col", swap(1, 4)))
    summed = plus(half, lax.ppermute(half, "col", swap(2, 4)))
    up_terms[3] = third_of(*stage[3])

    stage[1] = weights_of(1, False)
    piece_both = lax.ppermute(piece_chip, "col", swap(1, 4))
    stage[1] = second_of(*stage[1])
    up_terms[2] = weights_of(2, True)
    keep, send = gather(kept, place, [grad[q] for q in range(4)], w_up, True, False)
    half_in = plus(keep, lax.ppermute(send, "col", swap(1, 4)))
    arrived = lax.ppermute(half_in, "col", swap(2, 4))
    other = lax.ppermute(summed, "col", swap(1, 4))
    up_terms[1] = third_of(*stage[1])
    grad_down = down_weights(
        kept, place, ends, inner, grad_out, [piece, piece_core, piece_chip, piece_both], slots, factor
    )
    output = seat(place, summed, other)
    grad_up = join(place, (False, False, True, False), [
        up_terms[0], up_terms[1], up_terms[2], up_terms[3]], slots)
    summed_in = plus(half_in, arrived)
    other_in = lax.ppermute(summed_in, "col", swap(1, 4))
    grad_in = seat(place, summed_in, other_in)
    return (output, grad_in, grad_up, grad_down)


def solution(mesh):
    in_specs = (
        P("dp", "row"),
        P("row", "col", None, None),
        P("row", "col", None, None),
        P("row", "col"),
        P("dp", "row"),
    )
    out_specs = (
        P("dp", "row"),
        P("dp", "row"),
        P("row", "col", "dp", None),
        P("row", "col", "dp", None),
    )
    shape = dict(mesh.shape)
    lines_of_four = (shape["dp"], shape["row"], shape["col"]) == (4, 2, 4)
    return jax.shard_map(
        on_device if lines_of_four else on_any_mesh,
        mesh=mesh,
        in_specs=in_specs,
        out_specs=out_specs,
        check_vma=False,
    )
```

```python
import functools

import jax
import jax.numpy as jnp
from jax import lax
from jax.experimental import pallas as pl
from jax.experimental.pallas import tpu as pltpu
from jax.sharding import PartitionSpec as P


FF = 16384


CURVE = 0.7978845608028654
CUBIC = 0.044715


F32 = jnp.float32
BF16 = jnp.bfloat16


def activate(field):
    square = field * field
    tangent = jnp.tanh(field * (CURVE + CURVE * CUBIC * square))
    gate = 0.5 + 0.5 * tangent
    result = field * gate
    steepness = gate + result * (1.0 - tangent) * (CURVE + 3.0 * CURVE * CUBIC * square)
    return (result, steepness)


def column_lookup(kept_cols, columns):
    flattened = kept_cols.reshape(-1)
    return (flattened[:, None] == jnp.arange(columns, dtype=jnp.int32)[None, :]).astype(jnp.float32)


def spread_columns(blocks, lookup):
    row_count = blocks.shape[0]
    flattened = blocks.reshape(row_count, lookup.shape[0], blocks.shape[3])
    spread = jnp.einsum("tsf,sc->tcf", flattened, lookup, precision=lax.Precision.HIGHEST)
    return spread.reshape(row_count, -1)


def pick_columns(field, kept_cols, block_width):
    row_count = field.shape[0]
    reshaped = field.reshape(row_count, -1, block_width)
    picked = jnp.take(reshaped, kept_cols.reshape(-1), axis=1)
    return picked.reshape(row_count, kept_cols.shape[0], kept_cols.shape[1], block_width)


def on_any_mesh(tokens, w_up, w_down, kept_cols, grad_out):
    block_width = w_up.shape[2]
    token_count = tokens.shape[0]
    block_rows = w_up.shape[0]
    shard_columns = FF // (block_width * lax.axis_size("col"))
    tokens_cube = tokens.reshape(token_count, block_rows, block_width)
    grad_cube = grad_out.reshape(token_count, block_rows, block_width)
    lookup = column_lookup(kept_cols, shard_columns)
    factor = float(token_count * lax.axis_size("dp")) ** (-0.5)
    blocks = jnp.einsum("trb,rkbf->trkf", tokens_cube, w_up, preferred_element_type=jnp.float32)
    hidden_share = lax.psum_scatter(
        spread_columns(blocks, lookup).astype(jnp.bfloat16), "row", scatter_dimension=0, tiled=True
    ).astype(jnp.float32)
    act_value, act_slope = activate(hidden_share)
    act_share = act_value.astype(jnp.bfloat16)
    slope_share = act_slope.astype(jnp.bfloat16)
    act_all, slope_all = (
        lax.all_gather(act_share, "row", axis=0, tiled=True),
        lax.all_gather(slope_share, "row", axis=0, tiled=True),
    )
    act_picked = pick_columns(act_all, kept_cols, block_width)
    out_term = jnp.einsum("trkf,rkfd->trd", act_picked, w_down, preferred_element_type=jnp.float32)
    output = lax.psum(out_term.reshape(token_count, -1).astype(jnp.bfloat16), "col")
    back_blocks = jnp.einsum(
        "trd,rkfd->trkf", grad_cube, w_down, preferred_element_type=jnp.float32
    )
    back_all = lax.psum(spread_columns(back_blocks, lookup).astype(jnp.bfloat16), "row").astype(
        jnp.float32
    )
    hidden_grad = (back_all * slope_all).astype(jnp.bfloat16)
    grad_picked = pick_columns(hidden_grad, kept_cols, block_width)
    in_term = jnp.einsum("trkf,rkbf->trb", grad_picked, w_up, preferred_element_type=jnp.float32)
    grad_in = lax.psum(in_term.reshape(token_count, -1).astype(jnp.bfloat16), "col")
    up_weights = factor * jnp.einsum(
        "trb,trkf->rkbf", tokens_cube, grad_picked, preferred_element_type=jnp.float32
    )
    down_weights = factor * jnp.einsum(
        "trkf,trd->rkfd", act_picked, grad_cube, preferred_element_type=jnp.float32
    )
    grad_up, grad_down = (
        lax.psum_scatter(
            up_weights.astype(jnp.bfloat16), "dp", scatter_dimension=2, tiled=True
        ).astype(jnp.float32),
        lax.psum_scatter(
            down_weights.astype(jnp.bfloat16), "dp", scatter_dimension=2, tiled=True
        ).astype(jnp.float32),
    )
    return (output, grad_in, grad_up, grad_down)


QUARTERS = 4
DP, ROW, CORE, COL, FAR, OUTER = range(6)
LATE = (2,)
NN = (((1,), (0,)), ((), ()))
NT = (((1,), (1,)), ((), ()))


def dot(left, right, dims):
    return lax.dot_general(left, right, dims, preferred_element_type=F32)


def across(blocks):
    return jnp.concatenate([blocks[k] for k in range(blocks.shape[0])], axis=1)


def stacked(blocks):
    return blocks.reshape(blocks.shape[0] * blocks.shape[1], blocks.shape[2])


def whole_block(shape):
    return pl.BlockSpec(shape, lambda *_: (0,) * len(shape))


def call(kernel, grid, scalars, inputs, in_specs, out_shape, out_specs, scratch=(), mib=16):
    return pl.pallas_call(
        kernel,
        out_shape=out_shape,
        grid_spec=pltpu.PrefetchScalarGridSpec(
            num_scalar_prefetch=len(scalars),
            grid=grid,
            in_specs=in_specs,
            out_specs=out_specs,
            scratch_shapes=list(scratch),
        ),
        compiler_params=pltpu.CompilerParams(vmem_limit_bytes=mib * 1024 * 1024),
    )(*scalars, *inputs)


def spread_kernel(transposed, step, kept, place, x_ref, w_ref, *rest):
    outs, total = rest[:-1], rest[-1]
    slots, width = w_ref.shape[1], w_ref.shape[2]
    quarter = width // QUARTERS
    at = pl.program_id(0)

    @pl.when(at == 0)
    def _():
        total[...] = jnp.zeros_like(total)

    def row(i, carry):
        x = x_ref[:, pl.ds(pl.multiple_of(i * width, width), width)]
        if transposed:
            terms = dot(x, stacked(w_ref[i]), NT)
        else:
            terms = dot(x, across(w_ref[i]), NN)
        for k in range(slots):
            column = kept[(at * step + i) * slots + k]
            total[column] += terms[:, k * width:(k + 1) * width]
        return carry

    lax.fori_loop(0, step, row, 0, unroll=4)

    @pl.when(at == pl.num_programs(0) - 1)
    def _():
        def flip(column, carry):
            turned = total[column].astype(BF16).T
            quarters = [turned[q * quarter:(q + 1) * quarter] for q in range(QUARTERS)]
            if transposed:
                for q in range(QUARTERS):
                    outs[q][column] = quarters[q]
            else:
                far = place[FAR]
                outs[0][far, column] = quarters[0]
                outs[0][1 - far, column] = quarters[3]
                outs[1][far, column] = quarters[1]
                outs[1][1 - far, column] = quarters[2]
            return carry

        lax.fori_loop(0, total.shape[0], flip, 0, unroll=8)


def spread(kept, place, x, w, columns, transposed, step=8):
    rows, slots, width = w.shape[0], w.shape[1], w.shape[2]
    tokens = x.shape[0]
    shape = (columns, width // QUARTERS, tokens)
    shapes = [shape] * QUARTERS if transposed else [(2,) + shape] * 2
    return call(
        functools.partial(spread_kernel, transposed, step),
        (rows // step,),
        (kept, place),
        (x, w),
        [
            pl.BlockSpec((tokens, step * width), lambda g, *_: (0, g)),
            pl.BlockSpec((step, slots, width, width), lambda g, *_: (g, 0, 0, 0)),
        ],
        [jax.ShapeDtypeStruct(shape, BF16) for shape in shapes],
        [whole_block(shape) for shape in shapes],
        [pltpu.VMEM((columns, tokens, width), F32)],
    )


def activate_kernel(step, row_half, place, own_ref, sent_ref, *rest):
    halves_in, outs = (rest[:2], rest[2:]) if len(rest) == 8 else ((), rest)
    acts, halves, slopes = outs[:2], outs[2:-1], outs[-1]
    at = pl.program_id(0)
    start = at * step - place[ROW] * row_half

    def block(c, carry):
        pair = []
        for i in range(2):
            act, slope = activate(own_ref[i, c].astype(F32) + sent_ref[i, c].astype(F32))
            pair.append(act.astype(BF16))
            acts[i][c] = pair[i]
            slopes[i, c] = slope.astype(BF16)

        @pl.when((start >= 0) & (start < row_half))
        def _():
            if not halves_in:
                for i in range(2):
                    halves[i][start + c] = pair[i]
            else:
                near, far = halves_in[0][start + c], halves_in[1][start + c]
                outer = place[OUTER] == 1
                halves[0][start + c] = jnp.where(outer, pair[0], near)
                halves[1][start + c] = jnp.where(outer, pair[1], far)
                halves[2][start + c] = jnp.where(outer, far, pair[1])

        return carry

    lax.fori_loop(0, step, block, 0, unroll=4)


def activate_pair(place, own, sent, ends=(), step=8):
    _, columns, quarter, tokens = own.shape
    pair = pl.BlockSpec((2, step, quarter, tokens), lambda g, *_: (0, g, 0, 0))
    one = pl.BlockSpec((step, quarter, tokens), lambda g, *_: (g, 0, 0))
    half = (columns // 2, quarter, tokens)
    count = 3 if ends else 2
    return call(
        functools.partial(activate_kernel, step, columns // 2),
        (columns // step,),
        (place,),
        (own, sent, *ends),
        [pair, pair] + [whole_block(half)] * len(ends),
        [jax.ShapeDtypeStruct((columns, quarter, tokens), BF16)] * 2
        + [jax.ShapeDtypeStruct(half, BF16)] * count
        + [jax.ShapeDtypeStruct(own.shape, BF16)],
        [one] * 2 + [whole_block(half)] * count + [pair],
    )


def gather_kernel(transposed, mirrored, step, kept, place, *rest):
    parts, w_ref, keep_ref, send_ref, natural = (
        rest[:QUARTERS], rest[QUARTERS], rest[-3], rest[-2], rest[-1]
    )
    slots, width = w_ref.shape[1], w_ref.shape[2]
    half = keep_ref.shape[0]
    at = pl.program_id(0)

    def lay(order):
        def flip(column, carry):
            natural[column] = jnp.concatenate([part[column] for part in order], axis=0).T
            return carry

        lax.fori_loop(0, natural.shape[0], flip, 0, unroll=8)

    if mirrored:
        pl.when((at == 0) & (place[FAR] == 0))(lambda: lay(parts))
        pl.when((at == 0) & (place[FAR] == 1))(lambda: lay(parts[::-1]))
    else:
        pl.when(at == 0)(lambda: lay(parts))

    mine = pl.multiple_of(place[CORE] * half, half)
    other = pl.multiple_of((1 - place[CORE]) * half, half)

    def row(i, carry):
        columns = [kept[(at * step + i) * slots + k] for k in range(slots)]
        lanes = pl.ds(pl.multiple_of(i * width, width), width)
        for ref, start in ((keep_ref, mine), (send_ref, other)):
            left = jnp.concatenate([natural[c, pl.ds(start, half), :] for c in columns], axis=1)
            if transposed:
                term = dot(left, across(w_ref[i]), NT)
            else:
                term = dot(left, stacked(w_ref[i]), NN)
            ref[:, lanes] = term.astype(BF16)
        return carry

    lax.fori_loop(0, step, row, 0, unroll=4)


def gather(kept, place, parts, w, transposed, mirrored, step=8):
    rows, slots, width = w.shape[0], w.shape[1], w.shape[2]
    columns, quarter, tokens = parts[0].shape
    half = tokens // 2
    return call(
        functools.partial(gather_kernel, transposed, mirrored, step),
        (rows // step,),
        (kept, place),
        (*parts, w),
        [whole_block((columns, quarter, tokens))] * QUARTERS
        + [pl.BlockSpec((step, slots, width, width), lambda g, *_: (g, 0, 0, 0))],
        [jax.ShapeDtypeStruct((half, rows * width), BF16)] * 2,
        [pl.BlockSpec((half, step * width), lambda g, *_: (0, g))] * 2,
        [pltpu.VMEM((columns, tokens, width), BF16)],
    )


def up_weights_kernel(factor, direct, step, kept, place, own, sent, slope, tok_ref, *outs):
    grad_ref, outs = outs[0], outs[1:]
    quarter = grad_ref.shape[1]
    slots = outs[0].shape[-1] // quarter
    at = pl.program_id(0)

    @pl.when(at == 0)
    def _():
        def block(c, carry):
            grad = (own[c].astype(F32) + sent[c].astype(F32)) * slope[c].astype(F32)
            grad_ref[c] = grad.astype(BF16)
            return carry

        lax.fori_loop(0, own.shape[0], block, 0, unroll=4)

    if direct:
        owners = [jnp.bitwise_xor(place[DP], m) for m in range(QUARTERS)]
    else:
        owners = [jnp.where(place[FAR] == 0, m, 3 - m) for m in range(QUARTERS)]

    def row(i, carry):
        left = jnp.concatenate(
            [tok_ref[i, pl.ds(pl.multiple_of(m * quarter, quarter), quarter), :] for m in owners],
            axis=0,
        )
        right = jnp.concatenate(
            [grad_ref[kept[(at * step + i) * slots + k]] for k in range(slots)], axis=0
        )
        term = (factor * dot(left, right, NT)).astype(BF16)
        pieces = [term[m * quarter:(m + 1) * quarter] for m in range(QUARTERS)]
        outs[0][i] = pieces[0]
        for m in (1, 2, 3):
            if direct:
                outs[m][i] = pieces[m]
            else:
                outs[1][m - 1, i] = pieces[m]
        return carry

    lax.fori_loop(0, step, row, 0, unroll=4)


def up_weights(kept, place, q, direct, own, sent, slopes, tok_t, slots, factor, step=8):
    columns, quarter, tokens = own.shape
    rows, width = tok_t.shape[0], tok_t.shape[1]
    one = (rows, quarter, slots * quarter)
    one_spec = pl.BlockSpec((step,) + one[1:], lambda g, *_: (g, 0, 0))
    three_spec = pl.BlockSpec((3, step) + one[1:], lambda g, *_: (0, g, 0, 0))
    shapes = [one] * 4 if direct else [one, (3,) + one]

    def slope_index(g, kept, place):
        return (place[FAR] if q < 2 else 1 - place[FAR], 0, 0, 0)

    return call(
        functools.partial(up_weights_kernel, factor, direct, step),
        (rows // step,),
        (kept, place),
        (own, sent, slopes, tok_t),
        [whole_block((columns, quarter, tokens))] * 2
        + [pl.BlockSpec((None, columns, quarter, tokens), slope_index)]
        + [pl.BlockSpec((step, width, tokens), lambda g, *_: (g, 0, 0))],
        [jax.ShapeDtypeStruct((columns, quarter, tokens), BF16)]
        + [jax.ShapeDtypeStruct(shape, BF16) for shape in shapes],
        [whole_block((columns, quarter, tokens))]
        + ([one_spec] * 4 if direct else [one_spec, three_spec]),
    )


def join_kernel(kinds, place, *rest):
    terms, out_ref = rest[:-1], rest[-1]
    step, slots, quarter, width = out_ref.shape
    lane = lax.broadcasted_iota(jnp.int32, (quarter, width), 1) // quarter
    outer = place[OUTER] == 1

    def row(i, carry):
        sums, first = [], 0
        for direct in kinds:
            count = 4 if direct else 5
            group = [term[i].astype(F32) for term in terms[first:first + count]]
            first += count
            if direct:
                sums.append(group[0] + group[1] + group[2] + group[3])
            else:
                sums.append(jnp.where(outer, group[0] + group[1], group[2] + group[3] + group[4]))
        for k in range(slots):
            block = None
            for q in range(QUARTERS):
                shift = ((q - k) * quarter) % width
                piece = pltpu.roll(sums[q], shift, 1) if shift else sums[q]
                block = piece if block is None else jnp.where(lane == q, piece, block)
            out_ref[i, k] = block
        return carry

    lax.fori_loop(0, step, row, 0, unroll=4)


def join(place, kinds, parts, slots, step=8):
    rows, quarter, width = parts[0][0].shape
    terms = [term for part in parts for term in part]

    def spec(term):
        if len(term.shape) == 4:
            return pl.BlockSpec((None, step, quarter, width), lambda g, *_: (0, g, 0, 0))
        return pl.BlockSpec((step, quarter, width), lambda g, *_: (g, 0, 0))

    return call(
        functools.partial(join_kernel, kinds),
        (rows // step,),
        (place,),
        terms,
        [spec(term) for term in terms],
        jax.ShapeDtypeStruct((rows, slots, quarter, width), F32),
        pl.BlockSpec((step, slots, quarter, width), lambda g, *_: (g, 0, 0, 0)),
    )


def down_weights_kernel(factor, step, kept, place, *rest):
    ends, inner, got, given, own_ref, pieces, out_ref, wide = (
        rest[0], rest[1], rest[2:5], rest[5:8], rest[8], rest[9:21], rest[21], rest[22]
    )
    columns, quarter, tokens = ends.shape
    slots, width = out_ref.shape[1], out_ref.shape[3]
    m, at = pl.program_id(0), pl.program_id(1)
    start = (jnp.bitwise_xor(place[COL], m) * pl.num_programs(1) + at) * step

    def lay(act):
        def block(column, carry):
            wide[column, :, :tokens] = act[column]
            return carry

        lax.fori_loop(0, columns, block, 0, unroll=4)

    opening = (m == 0) & (at == 0)
    pl.when(opening & (place[OUTER] == 1))(lambda: lay(ends))
    pl.when(opening & (place[OUTER] == 0))(lambda: lay(inner))

    @pl.when(opening)
    def _():
        half = columns // 2

        def block(c, carry):
            for d in range(3):
                lanes = slice((d + 1) * tokens, (d + 2) * tokens)
                wide[place[ROW] * half + c, :, lanes] = got[d][c]
                wide[(1 - place[ROW]) * half + c, :, lanes] = given[d][c]
            return carry

        lax.fori_loop(0, half, block, 0, unroll=2)

    def work(others):
        def row(i, carry):
            lanes = pl.ds(pl.multiple_of(i * width, width), width)
            left = jnp.concatenate(
                [wide[kept[(start + i) * slots + k]] for k in range(slots)], axis=0
            )
            right = jnp.concatenate([own_ref[:, lanes]] + [other[:, lanes] for other in others], axis=0)
            out_ref[i] = (factor * dot(left, right, NN)).reshape(slots, quarter, width)
            return carry

        lax.fori_loop(0, step, row, 0, unroll=2)

    for index in range(4):
        pl.when(m == index)(functools.partial(work, pieces[3 * index:3 * index + 3]))


def down_weights(kept, place, ends, inner, got, given, own, pieces, slots, factor, step=8):
    columns, quarter, tokens = ends.shape
    width = slots * quarter
    rows = own.shape[1] // width
    shares = len(pieces) // 3
    steps = rows // (shares * step)

    def own_index(m, g, kept, place):
        return (0, jnp.bitwise_xor(place[COL], m) * steps + g)

    def out_index(m, g, kept, place):
        return (jnp.bitwise_xor(place[COL], m) * steps + g, 0, 0, 0)

    def piece_spec(index):
        def of(m, g, *_):
            return (0, jnp.where(m < index, 0, jnp.where(m > index, steps - 1, g)))

        return pl.BlockSpec((tokens, step * width), of)

    return call(
        functools.partial(down_weights_kernel, factor, step),
        (shares, steps),
        (kept, place),
        (ends, inner, *got, *given, own, *pieces),
        [whole_block((columns, quarter, tokens))] * 2
        + [whole_block(got[0].shape)] * 6
        + [pl.BlockSpec((tokens, step * width), own_index)]
        + [piece_spec(i // 3) for i in range(len(pieces))],
        jax.ShapeDtypeStruct((rows, slots, quarter, width), F32),
        pl.BlockSpec((step, slots, quarter, width), out_index),
        [pltpu.VMEM((columns, quarter, 4 * tokens), BF16)],
        mib=24,
    )


def seat_kernel(place, mine_ref, other_ref, out_ref):
    half = mine_ref.shape[0]
    out_ref[pl.ds(pl.multiple_of(place[CORE] * half, half), half), :] = mine_ref[...]
    out_ref[pl.ds(pl.multiple_of((1 - place[CORE]) * half, half), half), :] = other_ref[...]


def seat(place, mine, other, steps=4):
    half, width = mine.shape
    block = pl.BlockSpec((half, width // steps), lambda g, place: (0, g))
    return call(
        seat_kernel,
        (steps,),
        (place,),
        (mine, other),
        [block] * 2,
        jax.ShapeDtypeStruct((2 * half, width), BF16),
        pl.BlockSpec((2 * half, width // steps), lambda g, place: (0, g)),
    )


def swap(mask, size):
    return [(i, i ^ mask) for i in range(size)]


INWARD = [(0, 1), (3, 2)]
OUTWARD = [(1, 0), (2, 3)]
MIDDLE = [(1, 2), (2, 1)]


def plus(a, b):
    return (a.astype(F32) + b.astype(F32)).astype(BF16)


def on_device(tokens, w_up, w_down, kept_cols, grad_out):
    return layer(tokens, w_up, w_down, kept_cols, grad_out)


def layer(tokens, w_up, w_down, kept_cols, grad_out):
    width = w_up.shape[2]
    token_count = tokens.shape[0]
    rows, slots = w_up.shape[0], w_up.shape[1]
    columns = FF // (width * lax.axis_size("col"))
    factor = float(token_count * lax.axis_size("dp")) ** (-0.5)
    dp, row, col = lax.axis_index("dp"), lax.axis_index("row"), lax.axis_index("col")
    outer = jnp.where((dp == 0) | (dp == 3), 1, 0)
    kept = kept_cols.reshape(-1)
    place = jnp.stack([dp, row, col % 2, col, dp // 2, outer]).astype(jnp.int32)

    ends_own, inner_own = spread(kept, place, tokens, w_up, columns, False)
    back_own = spread(kept, place, grad_out, w_down, columns, True)
    ends_sent = lax.ppermute(ends_own, "row", swap(1, 2))
    inner_sent = lax.ppermute(inner_own, "row", swap(1, 2))
    back_sent = [lax.ppermute(back_own[q], "row", swap(1, 2)) for q in range(QUARTERS)]

    share = grad_out.shape[1] // 4
    mine = lax.dynamic_slice_in_dim(grad_out, col * share, share, axis=1)
    own_share = [lax.ppermute(mine, "dp", swap(d, 4)) for d in (1, 2, 3)]
    chip_share = [lax.ppermute(own_share[d], "col", swap(2, 4)) for d in range(3)]
    core_share = [lax.ppermute(own_share[d], "col", swap(1, 4)) for d in range(3)]
    both_share = [lax.ppermute(chip_share[d], "col", swap(1, 4)) for d in range(3)]
    pieces = own_share + core_share + chip_share + both_share

    end_near, end_far, *halves, end_slopes = activate_pair(place, ends_own, ends_sent)
    near, far, *sends, inner_slopes = activate_pair(place, inner_own, inner_sent, halves)
    got = [lax.ppermute(sends[d - 1], "dp", swap(d, 4)) for d in (1, 2, 3)]
    given = [lax.ppermute(got[d - 1], "row", swap(1, 2)) for d in (1, 2, 3)]

    keep, send = gather(kept, place, [end_near, near, far, end_far], w_down, False, True)
    half = plus(keep, lax.ppermute(send, "col", swap(1, 4)))
    summed = plus(half, lax.ppermute(half, "col", swap(2, 4)))
    other = lax.ppermute(summed, "col", swap(1, 4))
    output = seat(place, summed, other)

    tok_t = tokens.reshape(token_count, rows, width).transpose(1, 2, 0)
    grad, parts = [], []
    for q in range(QUARTERS):
        direct = q in LATE
        slopes = end_slopes if q in (0, 3) else inner_slopes
        hidden_grad, *terms = up_weights(
            kept, place, q, direct, back_own[q], back_sent[q], slopes, tok_t, slots, factor
        )
        grad.append(hidden_grad)
        if direct:
            parts.append([terms[0]] + [lax.ppermute(terms[m], "dp", swap(m, 4)) for m in (1, 2, 3)])
        else:
            home, rest = terms
            arrived = lax.ppermute(rest, "dp", INWARD)
            crossed = lax.ppermute(plus(rest[1:], arrived[1:]), "dp", MIDDLE)
            last = lax.ppermute(plus(home, crossed[1]), "dp", OUTWARD)
            parts.append([home, last, rest, arrived, crossed])

    keep, send = gather(kept, place, grad, w_up, True, False)
    half = plus(keep, lax.ppermute(send, "col", swap(1, 4)))
    summed = plus(half, lax.ppermute(half, "col", swap(2, 4)))
    other = lax.ppermute(summed, "col", swap(1, 4))
    grad_in = seat(place, summed, other)

    grad_down = down_weights(
        kept, place, end_near, near, got, given, grad_out, pieces, slots, factor
    )
    grad_up = join(place, tuple(q in LATE for q in range(QUARTERS)), parts, slots)
    return (output, grad_in, grad_up, grad_down)


def solution(mesh):
    in_specs = (
        P("dp", "row"),
        P("row", "col", None, None),
        P("row", "col", None, None),
        P("row", "col"),
        P("dp", "row"),
    )
    out_specs = (
        P("dp", "row"),
        P("dp", "row"),
        P("row", "col", "dp", None),
        P("row", "col", "dp", None),
    )
    shape = dict(mesh.shape)
    lines_of_four = (shape["dp"], shape["row"], shape["col"]) == (4, 2, 4)
    return jax.shard_map(
        on_device if lines_of_four else on_any_mesh,
        mesh=mesh,
        in_specs=in_specs,
        out_specs=out_specs,
        check_vma=False,
    )
```

```python
import functools

import jax
import jax.numpy as jnp
from jax import lax
from jax.experimental import pallas as pl
from jax.experimental.pallas import tpu as pltpu
from jax.sharding import PartitionSpec as P


FF = 16384


CURVE = 0.7978845608028654
CUBIC = 0.044715


F32 = jnp.float32
BF16 = jnp.bfloat16


def activate(field):
    square = field * field
    tangent = jnp.tanh(field * (CURVE + CURVE * CUBIC * square))
    gate = 0.5 + 0.5 * tangent
    result = field * gate
    steepness = gate + result * (1.0 - tangent) * (CURVE + 3.0 * CURVE * CUBIC * square)
    return (result, steepness)


def column_lookup(kept_cols, columns):
    flattened = kept_cols.reshape(-1)
    return (flattened[:, None] == jnp.arange(columns, dtype=jnp.int32)[None, :]).astype(jnp.float32)


def spread_columns(blocks, lookup):
    row_count = blocks.shape[0]
    flattened = blocks.reshape(row_count, lookup.shape[0], blocks.shape[3])
    spread = jnp.einsum("tsf,sc->tcf", flattened, lookup, precision=lax.Precision.HIGHEST)
    return spread.reshape(row_count, -1)


def pick_columns(field, kept_cols, block_width):
    row_count = field.shape[0]
    reshaped = field.reshape(row_count, -1, block_width)
    picked = jnp.take(reshaped, kept_cols.reshape(-1), axis=1)
    return picked.reshape(row_count, kept_cols.shape[0], kept_cols.shape[1], block_width)


def on_any_mesh(tokens, w_up, w_down, kept_cols, grad_out):
    block_width = w_up.shape[2]
    token_count = tokens.shape[0]
    block_rows = w_up.shape[0]
    shard_columns = FF // (block_width * lax.axis_size("col"))
    tokens_cube = tokens.reshape(token_count, block_rows, block_width)
    grad_cube = grad_out.reshape(token_count, block_rows, block_width)
    lookup = column_lookup(kept_cols, shard_columns)
    factor = float(token_count * lax.axis_size("dp")) ** (-0.5)
    blocks = jnp.einsum("trb,rkbf->trkf", tokens_cube, w_up, preferred_element_type=jnp.float32)
    hidden_share = lax.psum_scatter(
        spread_columns(blocks, lookup).astype(jnp.bfloat16), "row", scatter_dimension=0, tiled=True
    ).astype(jnp.float32)
    act_value, act_slope = activate(hidden_share)
    act_share = act_value.astype(jnp.bfloat16)
    slope_share = act_slope.astype(jnp.bfloat16)
    act_all, slope_all = (
        lax.all_gather(act_share, "row", axis=0, tiled=True),
        lax.all_gather(slope_share, "row", axis=0, tiled=True),
    )
    act_picked = pick_columns(act_all, kept_cols, block_width)
    out_term = jnp.einsum("trkf,rkfd->trd", act_picked, w_down, preferred_element_type=jnp.float32)
    output = lax.psum(out_term.reshape(token_count, -1).astype(jnp.bfloat16), "col")
    back_blocks = jnp.einsum(
        "trd,rkfd->trkf", grad_cube, w_down, preferred_element_type=jnp.float32
    )
    back_all = lax.psum(spread_columns(back_blocks, lookup).astype(jnp.bfloat16), "row").astype(
        jnp.float32
    )
    hidden_grad = (back_all * slope_all).astype(jnp.bfloat16)
    grad_picked = pick_columns(hidden_grad, kept_cols, block_width)
    in_term = jnp.einsum("trkf,rkbf->trb", grad_picked, w_up, preferred_element_type=jnp.float32)
    grad_in = lax.psum(in_term.reshape(token_count, -1).astype(jnp.bfloat16), "col")
    up_weights = factor * jnp.einsum(
        "trb,trkf->rkbf", tokens_cube, grad_picked, preferred_element_type=jnp.float32
    )
    down_weights = factor * jnp.einsum(
        "trkf,trd->rkfd", act_picked, grad_cube, preferred_element_type=jnp.float32
    )
    grad_up, grad_down = (
        lax.psum_scatter(
            up_weights.astype(jnp.bfloat16), "dp", scatter_dimension=2, tiled=True
        ).astype(jnp.float32),
        lax.psum_scatter(
            down_weights.astype(jnp.bfloat16), "dp", scatter_dimension=2, tiled=True
        ).astype(jnp.float32),
    )
    return (output, grad_in, grad_up, grad_down)


QUARTERS = 4
DP, ROW, CORE, COL, FAR, OUTER = range(6)
LATE = (2, 3)
NN = (((1,), (0,)), ((), ()))
NT = (((1,), (1,)), ((), ()))


def dot(left, right, dims):
    return lax.dot_general(left, right, dims, preferred_element_type=F32)


def across(blocks):
    return jnp.concatenate([blocks[k] for k in range(blocks.shape[0])], axis=1)


def stacked(blocks):
    return blocks.reshape(blocks.shape[0] * blocks.shape[1], blocks.shape[2])


def whole_block(shape):
    return pl.BlockSpec(shape, lambda *_: (0,) * len(shape))


def call(kernel, grid, scalars, inputs, in_specs, out_shape, out_specs, scratch=(), mib=16):
    return pl.pallas_call(
        kernel,
        out_shape=out_shape,
        grid_spec=pltpu.PrefetchScalarGridSpec(
            num_scalar_prefetch=len(scalars),
            grid=grid,
            in_specs=in_specs,
            out_specs=out_specs,
            scratch_shapes=list(scratch),
        ),
        compiler_params=pltpu.CompilerParams(vmem_limit_bytes=mib * 1024 * 1024),
    )(*scalars, *inputs)


def spread_kernel(transposed, step, kept, place, x_ref, w_ref, *rest):
    outs, total = rest[:-1], rest[-1]
    slots, width = w_ref.shape[1], w_ref.shape[2]
    quarter = width // QUARTERS
    at = pl.program_id(0)

    @pl.when(at == 0)
    def _():
        total[...] = jnp.zeros_like(total)

    def row(i, carry):
        x = x_ref[:, pl.ds(pl.multiple_of(i * width, width), width)]
        if transposed:
            terms = dot(x, stacked(w_ref[i]), NT)
        else:
            terms = dot(x, across(w_ref[i]), NN)
        for k in range(slots):
            column = kept[(at * step + i) * slots + k]
            total[column] += terms[:, k * width:(k + 1) * width]
        return carry

    lax.fori_loop(0, step, row, 0, unroll=4)

    @pl.when(at == pl.num_programs(0) - 1)
    def _():
        def flip(column, carry):
            turned = total[column].astype(BF16).T
            quarters = [turned[q * quarter:(q + 1) * quarter] for q in range(QUARTERS)]
            if transposed:
                for q in range(QUARTERS):
                    outs[q][column] = quarters[q]
            else:
                far = place[FAR]
                outs[0][far, column] = quarters[0]
                outs[0][1 - far, column] = quarters[3]
                outs[1][far, column] = quarters[1]
                outs[1][1 - far, column] = quarters[2]
            return carry

        lax.fori_loop(0, total.shape[0], flip, 0, unroll=8)


def spread(kept, place, x, w, columns, transposed, step=8):
    rows, slots, width = w.shape[0], w.shape[1], w.shape[2]
    tokens = x.shape[0]
    shape = (columns, width // QUARTERS, tokens)
    shapes = [shape] * QUARTERS if transposed else [(2,) + shape] * 2
    return call(
        functools.partial(spread_kernel, transposed, step),
        (rows // step,),
        (kept, place),
        (x, w),
        [
            pl.BlockSpec((tokens, step * width), lambda g, *_: (0, g)),
            pl.BlockSpec((step, slots, width, width), lambda g, *_: (g, 0, 0, 0)),
        ],
        [jax.ShapeDtypeStruct(shape, BF16) for shape in shapes],
        [whole_block(shape) for shape in shapes],
        [pltpu.VMEM((columns, tokens, width), F32)],
    )


def activate_kernel(step, row_half, place, own_ref, sent_ref, *rest):
    halves_in, outs = (rest[:2], rest[2:]) if len(rest) == 8 else ((), rest)
    acts, halves, slopes = outs[:2], outs[2:-1], outs[-1]
    at = pl.program_id(0)
    start = at * step - place[ROW] * row_half

    def block(c, carry):
        pair = []
        for i in range(2):
            act, slope = activate(own_ref[i, c].astype(F32) + sent_ref[i, c].astype(F32))
            pair.append(act.astype(BF16))
            acts[i][c] = pair[i]
            slopes[i, c] = slope.astype(BF16)

        @pl.when((start >= 0) & (start < row_half))
        def _():
            if not halves_in:
                for i in range(2):
                    halves[i][start + c] = pair[i]
            else:
                near, far = halves_in[0][start + c], halves_in[1][start + c]
                outer = place[OUTER] == 1
                halves[0][start + c] = jnp.where(outer, pair[0], near)
                halves[1][start + c] = jnp.where(outer, pair[1], far)
                halves[2][start + c] = jnp.where(outer, far, pair[1])

        return carry

    lax.fori_loop(0, step, block, 0, unroll=4)


def activate_pair(place, own, sent, ends=(), step=8):
    _, columns, quarter, tokens = own.shape
    pair = pl.BlockSpec((2, step, quarter, tokens), lambda g, *_: (0, g, 0, 0))
    one = pl.BlockSpec((step, quarter, tokens), lambda g, *_: (g, 0, 0))
    half = (columns // 2, quarter, tokens)
    count = 3 if ends else 2
    return call(
        functools.partial(activate_kernel, step, columns // 2),
        (columns // step,),
        (place,),
        (own, sent, *ends),
        [pair, pair] + [whole_block(half)] * len(ends),
        [jax.ShapeDtypeStruct((columns, quarter, tokens), BF16)] * 2
        + [jax.ShapeDtypeStruct(half, BF16)] * count
        + [jax.ShapeDtypeStruct(own.shape, BF16)],
        [one] * 2 + [whole_block(half)] * count + [pair],
    )


def gather_kernel(transposed, mirrored, step, kept, place, *rest):
    parts, w_ref, keep_ref, send_ref, natural = (
        rest[:QUARTERS], rest[QUARTERS], rest[-3], rest[-2], rest[-1]
    )
    slots, width = w_ref.shape[1], w_ref.shape[2]
    half = keep_ref.shape[0]
    at = pl.program_id(0)

    def lay(order):
        def flip(column, carry):
            natural[column] = jnp.concatenate([part[column] for part in order], axis=0).T
            return carry

        lax.fori_loop(0, natural.shape[0], flip, 0, unroll=8)

    if mirrored:
        pl.when((at == 0) & (place[FAR] == 0))(lambda: lay(parts))
        pl.when((at == 0) & (place[FAR] == 1))(lambda: lay(parts[::-1]))
    else:
        pl.when(at == 0)(lambda: lay(parts))

    mine = pl.multiple_of(place[CORE] * half, half)
    other = pl.multiple_of((1 - place[CORE]) * half, half)

    def row(i, carry):
        columns = [kept[(at * step + i) * slots + k] for k in range(slots)]
        lanes = pl.ds(pl.multiple_of(i * width, width), width)
        for ref, start in ((keep_ref, mine), (send_ref, other)):
            left = jnp.concatenate([natural[c, pl.ds(start, half), :] for c in columns], axis=1)
            if transposed:
                term = dot(left, across(w_ref[i]), NT)
            else:
                term = dot(left, stacked(w_ref[i]), NN)
            ref[:, lanes] = term.astype(BF16)
        return carry

    lax.fori_loop(0, step, row, 0, unroll=8)


def gather(kept, place, parts, w, transposed, mirrored, step=8):
    rows, slots, width = w.shape[0], w.shape[1], w.shape[2]
    columns, quarter, tokens = parts[0].shape
    half = tokens // 2
    return call(
        functools.partial(gather_kernel, transposed, mirrored, step),
        (rows // step,),
        (kept, place),
        (*parts, w),
        [whole_block((columns, quarter, tokens))] * QUARTERS
        + [pl.BlockSpec((step, slots, width, width), lambda g, *_: (g, 0, 0, 0))],
        [jax.ShapeDtypeStruct((half, rows * width), BF16)] * 2,
        [pl.BlockSpec((half, step * width), lambda g, *_: (0, g))] * 2,
        [pltpu.VMEM((columns, tokens, width), BF16)],
    )


def up_weights_kernel(factor, direct, step, kept, place, own, sent, slope, tok_ref, *outs):
    grad_ref, outs = outs[0], outs[1:]
    quarter = grad_ref.shape[1]
    slots = outs[0].shape[-1] // quarter
    at = pl.program_id(0)

    @pl.when(at == 0)
    def _():
        def block(c, carry):
            grad = (own[c].astype(F32) + sent[c].astype(F32)) * slope[c].astype(F32)
            grad_ref[c] = grad.astype(BF16)
            return carry

        lax.fori_loop(0, own.shape[0], block, 0, unroll=4)

    if direct:
        owners = [jnp.bitwise_xor(place[DP], m) for m in range(QUARTERS)]
    else:
        owners = [jnp.where(place[FAR] == 0, m, 3 - m) for m in range(QUARTERS)]

    def row(i, carry):
        left = jnp.concatenate(
            [tok_ref[i, pl.ds(pl.multiple_of(m * quarter, quarter), quarter), :] for m in owners],
            axis=0,
        )
        right = jnp.concatenate(
            [grad_ref[kept[(at * step + i) * slots + k]] for k in range(slots)], axis=0
        )
        term = (factor * dot(left, right, NT)).astype(BF16)
        pieces = [term[m * quarter:(m + 1) * quarter] for m in range(QUARTERS)]
        outs[0][i] = pieces[0]
        for m in (1, 2, 3):
            if direct:
                outs[m][i] = pieces[m]
            else:
                outs[1][m - 1, i] = pieces[m]
        return carry

    lax.fori_loop(0, step, row, 0, unroll=8)


def up_weights(kept, place, q, direct, own, sent, slopes, tok_t, slots, factor, step=8):
    columns, quarter, tokens = own.shape
    rows, width = tok_t.shape[0], tok_t.shape[1]
    one = (rows, quarter, slots * quarter)
    one_spec = pl.BlockSpec((step,) + one[1:], lambda g, *_: (g, 0, 0))
    three_spec = pl.BlockSpec((3, step) + one[1:], lambda g, *_: (0, g, 0, 0))
    shapes = [one] * 4 if direct else [one, (3,) + one]

    def slope_index(g, kept, place):
        return (place[FAR] if q < 2 else 1 - place[FAR], 0, 0, 0)

    return call(
        functools.partial(up_weights_kernel, factor, direct, step),
        (rows // step,),
        (kept, place),
        (own, sent, slopes, tok_t),
        [whole_block((columns, quarter, tokens))] * 2
        + [pl.BlockSpec((None, columns, quarter, tokens), slope_index)]
        + [pl.BlockSpec((step, width, tokens), lambda g, *_: (g, 0, 0))],
        [jax.ShapeDtypeStruct((columns, quarter, tokens), BF16)]
        + [jax.ShapeDtypeStruct(shape, BF16) for shape in shapes],
        [whole_block((columns, quarter, tokens))]
        + ([one_spec] * 4 if direct else [one_spec, three_spec]),
    )


def join_kernel(kinds, place, *rest):
    terms, out_ref = rest[:-1], rest[-1]
    step, slots, quarter, width = out_ref.shape
    lane = lax.broadcasted_iota(jnp.int32, (quarter, width), 1) // quarter
    outer = place[OUTER] == 1

    def row(i, carry):
        sums, first = [], 0
        for direct in kinds:
            count = 4 if direct else 5
            group = [term[i].astype(F32) for term in terms[first:first + count]]
            first += count
            if direct:
                sums.append(group[0] + group[1] + group[2] + group[3])
            else:
                sums.append(jnp.where(outer, group[0] + group[1], group[2] + group[3] + group[4]))
        for k in range(slots):
            block = None
            for q in range(QUARTERS):
                shift = ((q - k) * quarter) % width
                piece = pltpu.roll(sums[q], shift, 1) if shift else sums[q]
                block = piece if block is None else jnp.where(lane == q, piece, block)
            out_ref[i, k] = block
        return carry

    lax.fori_loop(0, step, row, 0, unroll=4)


def join(place, kinds, parts, slots, step=8):
    rows, quarter, width = parts[0][0].shape
    terms = [term for part in parts for term in part]

    def spec(term):
        if len(term.shape) == 4:
            return pl.BlockSpec((None, step, quarter, width), lambda g, *_: (0, g, 0, 0))
        return pl.BlockSpec((step, quarter, width), lambda g, *_: (g, 0, 0))

    return call(
        functools.partial(join_kernel, kinds),
        (rows // step,),
        (place,),
        terms,
        [spec(term) for term in terms],
        jax.ShapeDtypeStruct((rows, slots, quarter, width), F32),
        pl.BlockSpec((step, slots, quarter, width), lambda g, *_: (g, 0, 0, 0)),
    )


def down_weights_kernel(factor, step, kept, place, *rest):
    ends, inner, got, given, own_ref, pieces, out_ref, wide = (
        rest[0], rest[1], rest[2:5], rest[5:8], rest[8], rest[9:21], rest[21], rest[22]
    )
    columns, quarter, tokens = ends.shape
    slots, width = out_ref.shape[1], out_ref.shape[3]
    m, at = pl.program_id(0), pl.program_id(1)
    start = (jnp.bitwise_xor(place[COL], m) * pl.num_programs(1) + at) * step

    def lay(act):
        def block(column, carry):
            wide[column, :, :tokens] = act[column]
            return carry

        lax.fori_loop(0, columns, block, 0, unroll=4)

    opening = (m == 0) & (at == 0)
    pl.when(opening & (place[OUTER] == 1))(lambda: lay(ends))
    pl.when(opening & (place[OUTER] == 0))(lambda: lay(inner))

    @pl.when(opening)
    def _():
        half = columns // 2

        def block(c, carry):
            for d in range(3):
                lanes = slice((d + 1) * tokens, (d + 2) * tokens)
                wide[place[ROW] * half + c, :, lanes] = got[d][c]
                wide[(1 - place[ROW]) * half + c, :, lanes] = given[d][c]
            return carry

        lax.fori_loop(0, half, block, 0, unroll=2)

    def work(others):
        def row(i, carry):
            lanes = pl.ds(pl.multiple_of(i * width, width), width)
            left = jnp.concatenate(
                [wide[kept[(start + i) * slots + k]] for k in range(slots)], axis=0
            )
            right = jnp.concatenate([own_ref[:, lanes]] + [other[:, lanes] for other in others], axis=0)
            out_ref[i] = (factor * dot(left, right, NN)).reshape(slots, quarter, width)
            return carry

        lax.fori_loop(0, step, row, 0, unroll=2)

    for index in range(4):
        pl.when(m == index)(functools.partial(work, pieces[3 * index:3 * index + 3]))


def down_weights(kept, place, ends, inner, got, given, own, pieces, slots, factor, step=8):
    columns, quarter, tokens = ends.shape
    width = slots * quarter
    rows = own.shape[1] // width
    shares = len(pieces) // 3
    steps = rows // (shares * step)

    def own_index(m, g, kept, place):
        return (0, jnp.bitwise_xor(place[COL], m) * steps + g)

    def out_index(m, g, kept, place):
        return (jnp.bitwise_xor(place[COL], m) * steps + g, 0, 0, 0)

    def piece_spec(index):
        def of(m, g, *_):
            return (0, jnp.where(m < index, 0, jnp.where(m > index, steps - 1, g)))

        return pl.BlockSpec((tokens, step * width), of)

    return call(
        functools.partial(down_weights_kernel, factor, step),
        (shares, steps),
        (kept, place),
        (ends, inner, *got, *given, own, *pieces),
        [whole_block((columns, quarter, tokens))] * 2
        + [whole_block(got[0].shape)] * 6
        + [pl.BlockSpec((tokens, step * width), own_index)]
        + [piece_spec(i // 3) for i in range(len(pieces))],
        jax.ShapeDtypeStruct((rows, slots, quarter, width), F32),
        pl.BlockSpec((step, slots, quarter, width), out_index),
        [pltpu.VMEM((columns, quarter, 4 * tokens), BF16)],
        mib=24,
    )


def seat_kernel(place, mine_ref, other_ref, out_ref):
    half = mine_ref.shape[0]
    out_ref[pl.ds(pl.multiple_of(place[CORE] * half, half), half), :] = mine_ref[...]
    out_ref[pl.ds(pl.multiple_of((1 - place[CORE]) * half, half), half), :] = other_ref[...]


def seat(place, mine, other, steps=4):
    half, width = mine.shape
    block = pl.BlockSpec((half, width // steps), lambda g, place: (0, g))
    return call(
        seat_kernel,
        (steps,),
        (place,),
        (mine, other),
        [block] * 2,
        jax.ShapeDtypeStruct((2 * half, width), BF16),
        pl.BlockSpec((2 * half, width // steps), lambda g, place: (0, g)),
    )


def swap(mask, size):
    return [(i, i ^ mask) for i in range(size)]


INWARD = [(0, 1), (3, 2)]
OUTWARD = [(1, 0), (2, 3)]
MIDDLE = [(1, 2), (2, 1)]


def plus(a, b):
    return (a.astype(F32) + b.astype(F32)).astype(BF16)


def on_device(tokens, w_up, w_down, kept_cols, grad_out):
    return layer(tokens, w_up, w_down, kept_cols, grad_out)


def layer(tokens, w_up, w_down, kept_cols, grad_out):
    width = w_up.shape[2]
    token_count = tokens.shape[0]
    rows, slots = w_up.shape[0], w_up.shape[1]
    columns = FF // (width * lax.axis_size("col"))
    factor = float(token_count * lax.axis_size("dp")) ** (-0.5)
    dp, row, col = lax.axis_index("dp"), lax.axis_index("row"), lax.axis_index("col")
    outer = jnp.where((dp == 0) | (dp == 3), 1, 0)
    kept = kept_cols.reshape(-1)
    place = jnp.stack([dp, row, col % 2, col, dp // 2, outer]).astype(jnp.int32)

    ends_own, inner_own = spread(kept, place, tokens, w_up, columns, False)
    back_own = spread(kept, place, grad_out, w_down, columns, True)
    ends_sent = lax.ppermute(ends_own, "row", swap(1, 2))
    inner_sent = lax.ppermute(inner_own, "row", swap(1, 2))
    back_sent = [lax.ppermute(back_own[q], "row", swap(1, 2)) for q in range(QUARTERS)]

    share = grad_out.shape[1] // 4
    mine = lax.dynamic_slice_in_dim(grad_out, col * share, share, axis=1)
    own_share = [lax.ppermute(mine, "dp", swap(d, 4)) for d in (1, 2, 3)]
    chip_share = [lax.ppermute(own_share[d], "col", swap(2, 4)) for d in range(3)]
    core_share = [lax.ppermute(own_share[d], "col", swap(1, 4)) for d in range(3)]
    both_share = [lax.ppermute(chip_share[d], "col", swap(1, 4)) for d in range(3)]
    pieces = own_share + core_share + chip_share + both_share

    end_near, end_far, *halves, end_slopes = activate_pair(place, ends_own, ends_sent)
    near, far, *sends, inner_slopes = activate_pair(place, inner_own, inner_sent, halves)
    got = [lax.ppermute(sends[d - 1], "dp", swap(d, 4)) for d in (1, 2, 3)]
    given = [lax.ppermute(got[d - 1], "row", swap(1, 2)) for d in (1, 2, 3)]

    keep, send = gather(kept, place, [end_near, near, far, end_far], w_down, False, True)
    half = plus(keep, lax.ppermute(send, "col", swap(1, 4)))
    summed = plus(half, lax.ppermute(half, "col", swap(2, 4)))
    other = lax.ppermute(summed, "col", swap(1, 4))
    output = seat(place, summed, other)

    tok_t = tokens.reshape(token_count, rows, width).transpose(1, 2, 0)
    grad, parts = [], []
    for q in range(QUARTERS):
        direct = q in LATE
        slopes = end_slopes if q in (0, 3) else inner_slopes
        hidden_grad, *terms = up_weights(
            kept, place, q, direct, back_own[q], back_sent[q], slopes, tok_t, slots, factor
        )
        grad.append(hidden_grad)
        if direct:
            parts.append([terms[0]] + [lax.ppermute(terms[m], "dp", swap(m, 4)) for m in (1, 2, 3)])
        else:
            home, rest = terms
            arrived = lax.ppermute(rest, "dp", INWARD)
            crossed = lax.ppermute(plus(rest[1:], arrived[1:]), "dp", MIDDLE)
            last = lax.ppermute(plus(home, crossed[1]), "dp", OUTWARD)
            parts.append([home, last, rest, arrived, crossed])

    keep, send = gather(kept, place, grad, w_up, True, False)
    half = plus(keep, lax.ppermute(send, "col", swap(1, 4)))
    summed = plus(half, lax.ppermute(half, "col", swap(2, 4)))
    other = lax.ppermute(summed, "col", swap(1, 4))
    grad_in = seat(place, summed, other)

    grad_down = down_weights(
        kept, place, end_near, near, got, given, grad_out, pieces, slots, factor
    )
    grad_up = join(place, tuple(q in LATE for q in range(QUARTERS)), parts, slots)
    return (output, grad_in, grad_up, grad_down)


def solution(mesh):
    in_specs = (
        P("dp", "row"),
        P("row", "col", None, None),
        P("row", "col", None, None),
        P("row", "col"),
        P("dp", "row"),
    )
    out_specs = (
        P("dp", "row"),
        P("dp", "row"),
        P("row", "col", "dp", None),
        P("row", "col", "dp", None),
    )
    shape = dict(mesh.shape)
    lines_of_four = (shape["dp"], shape["row"], shape["col"]) == (4, 2, 4)
    return jax.shard_map(
        on_device if lines_of_four else on_any_mesh,
        mesh=mesh,
        in_specs=in_specs,
        out_specs=out_specs,
        check_vma=False,
    )
```
